32 devices in a mesh: member: 8 (over z, x), tensor: 4 (over y, core).
Axes of the slice: x: 2, y: 2, z: 4, core: 2. Of those that a mesh axis runs over, the one named last changes fastest.
Arguments:
- tokens: bfloat16 [1024, 8192], P('member'), may hold values from -6 to 6
- out_grad: bfloat16 [1024, 8192], P('member'), may hold values from -6 to 6
- flip_bits: int32 [1024], P('member'), may hold values 0 or 1
- in_scale: float32 [8, 8192], P(None, 'member'), may hold values from 0.5 to 2
- out_scale: float32 [8, 8192], P(None, 'member'), may hold values from 0.5 to 2
- gate_scale: float32 [8, 14336], P('member', 'tensor'), may hold values from 0.5 to 2
- gate_flip: float32 [8, 14336], P('member', 'tensor'), may hold values from -2 to 2
- up_scale: float32 [8, 14336], P('member', 'tensor'), may hold values from 0.5 to 2
- up_flip: float32 [8, 14336], P('member', 'tensor'), may hold values from -2 to 2
- proj_gate: bfloat16 [1024, 14336], P('member', 'tensor'), may hold values from -6 to 6
- proj_up: bfloat16 [1024, 14336], P('member', 'tensor'), may hold values from -6 to 6
- w_gate: bfloat16 [8192, 14336], P('member', 'tensor'), may hold values from -0.0625 to 0.0625
- w_up: bfloat16 [8192, 14336], P('member', 'tensor'), may hold values from -0.0625 to 0.0625
- w_down: bfloat16 [14336, 8192], P('tensor', 'member'), may hold values from -0.046875 to 0.046875
Outputs:
- x_grad: bfloat16 [1024, 8192], P(('member', 'tensor'))
- w_gate_grad: bfloat16 [8192, 14336], P('member', 'tensor')
- w_up_grad: bfloat16 [8192, 14336], P('member', 'tensor')
- w_down_grad: bfloat16 [14336, 8192], P('tensor', 'member')
- in_scale_grad: float32 [8, 8192], P(None, 'member')
- out_scale_grad: float32 [8, 8192], P(None, 'member')
- gate_scale_grad: float32 [8, 14336], P('member', 'tensor')
- gate_flip_grad: float32 [8, 14336], P('member', 'tensor')
- up_scale_grad: float32 [8, 14336], P('member', 'tensor')
- up_flip_grad: float32 [8, 14336], P('member', 'tensor')
The draws below stay inside these ranges and needn't reach their ends.
All inputs are finite; a program needn't handle non-finite values. No bound on the sum of `flip_bits` on one device may be relied on, other than what follows from the above.
Results may differ from the reference program's by a relative error of at most 0.024.
Values may be sent and summed in bfloat16 or wider, within the bound.
A program may use at most 128 MiB of HBM per device.

```python
import math
import jax
import jax.numpy as jnp

D = 8192
FF = 14336
TOK = 128
MEMBERS = 8
TOKENS = 1024


def touch_ends(result, key, low, high):
    place = [jax.random.randint(jax.random.fold_in(key, axis), (), 0, length) for axis, length in enumerate(result.shape)]
    main_axis = result.shape.index(max(result.shape))
    neighbour = place[:main_axis] + [(place[main_axis] + 1) % result.shape[main_axis]] + place[main_axis + 1:]
    return result.at[tuple(place)].set(low).at[tuple(neighbour)].set(high)


def shard_levels(own_key, shape, cuts, smallest, largest):
    level, own = 1.0, jax.random.fold_in(own_key, 6)
    for position, parts in cuts:
        draws = jnp.exp(jax.random.uniform(jax.random.fold_in(own, position), (parts,), jnp.float32, smallest / len(cuts), largest / len(cuts)))
        level = level * jnp.repeat(draws, shape[position] // parts).reshape([-1 if axis == position else 1 for axis in range(len(shape))])
    return level


def centred(key, extent, width, reach, pieces=(), kind=jnp.bfloat16):
    array = jax.random.normal(key, extent, jnp.float32) * width
    if len(pieces) > 0:
        array = shard_levels(key, extent, pieces, -0.22, 0.18) * array
    return jnp.clip(array, min=-reach, max=reach).astype(kind)


def setup_inputs(seed: int = 0) -> dict:
    splits = jax.random.split(jax.random.key(seed), 15)
    tokens = centred(splits[0], (TOKENS, D), 1.0, 6.0, ((0, 8),))
    out_grad = centred(splits[1], (TOKENS, D), 1.0, 6.0, ((0, 8),))
    flip_bits = touch_ends((jax.random.randint(splits[2], (TOKENS,), 0, 2) < 1).astype(jnp.int32), jax.random.fold_in(splits[2], 1), 0, 1)
    in_scale = jnp.clip(jnp.exp(math.log(2.0) - 1.3862944 * jax.random.uniform(splits[3], (MEMBERS, D), jnp.float32) ** shard_levels(splits[3], (MEMBERS, D), ((1, 8),), -0.2, 0.2)), 0.5, 2.0)
    out_scale = jnp.clip(jnp.exp(math.log(2.0) - 1.3862944 * jax.random.uniform(splits[4], (MEMBERS, D), jnp.float32) ** shard_levels(splits[4], (MEMBERS, D), ((1, 8),), -0.2, 0.2)), 0.5, 2.0)
    gate_scale = jnp.clip(jnp.exp(math.log(2.0) - 1.3862944 * jax.random.uniform(splits[5], (MEMBERS, FF), jnp.float32) ** shard_levels(splits[5], (MEMBERS, FF), ((0, 8), (1, 4)), -0.2, 0.2)), 0.5, 2.0)
    gate_flip = centred(splits[6], (MEMBERS, FF), 0.5, 2.0, ((0, 8), (1, 4)), jnp.float32)
    up_scale = jnp.clip(jnp.exp(math.log(2.0) - 1.3862944 * jax.random.uniform(splits[7], (MEMBERS, FF), jnp.float32) ** shard_levels(splits[7], (MEMBERS, FF), ((0, 8), (1, 4)), -0.2, 0.2)), 0.5, 2.0)
    up_flip = centred(splits[8], (MEMBERS, FF), 0.5, 2.0, ((0, 8), (1, 4)), jnp.float32)
    proj_gate = centred(splits[9], (TOKENS, FF), 1.0, 6.0, ((0, 8), (1, 4)))
    proj_up = centred(splits[10], (TOKENS, FF), 1.0, 6.0, ((0, 8), (1, 4)))
    w_gate = centred(splits[11], (D, FF), D ** -0.5, 0.0625, ((0, 8), (1, 4)))
    w_up = centred(splits[12], (D, FF), D ** -0.5, 0.0625, ((0, 8), (1, 4)))
    w_down = centred(splits[13], (FF, D), FF ** -0.5, 0.046875, ((0, 4), (1, 8)))
    return dict(tokens=tokens, out_grad=out_grad, flip_bits=flip_bits, in_scale=in_scale, out_scale=out_scale, gate_scale=gate_scale, gate_flip=gate_flip, up_scale=up_scale, up_flip=up_flip, proj_gate=proj_gate, proj_up=proj_up, w_gate=w_gate, w_up=w_up, w_down=w_down)


def per_member(values):
    return values.reshape(MEMBERS, TOK, values.shape[-1]).sum(axis=1)


def reference(tokens, out_grad, flip_bits, in_scale, out_scale, gate_scale, gate_flip, up_scale, up_flip, proj_gate, proj_up, w_gate, w_up, w_down):
    def spread(table):
        return jnp.repeat(table, TOK, axis=0)

    sign = (2 * flip_bits - 1).astype(jnp.float32)[:, None]
    gate_factor = spread(gate_scale) + sign * spread(gate_flip)
    up_factor = spread(up_scale) + sign * spread(up_flip)
    pg_f = proj_gate.astype(jnp.float32)
    pu_f = proj_up.astype(jnp.float32)
    gate = pg_f * gate_factor
    up = pu_f * up_factor
    sig = jax.nn.sigmoid(gate)
    act = gate * sig
    hidden = (act * up).astype(jnp.bfloat16)
    in_rows = (tokens.astype(jnp.float32) * spread(in_scale)).astype(jnp.bfloat16)
    grad_z = (out_grad.astype(jnp.float32) * spread(out_scale)).astype(jnp.bfloat16)
    grad_hidden = jnp.dot(grad_z, w_down.T, preferred_element_type=jnp.float32)
    grad_gate = grad_hidden * up * sig * (1.0 + gate * (1.0 - sig))
    grad_up = grad_hidden * act
    gate_scale_grad = per_member(grad_gate * pg_f)
    gate_flip_grad = per_member(sign * grad_gate * pg_f)
    up_scale_grad = per_member(grad_up * pu_f)
    up_flip_grad = per_member(sign * grad_up * pu_f)
    grad_pg = (grad_gate * gate_factor).astype(jnp.bfloat16)
    grad_pu = (grad_up * up_factor).astype(jnp.bfloat16)
    w_gate_grad = jnp.dot(in_rows.T, grad_pg, preferred_element_type=jnp.float32).astype(jnp.bfloat16)
    w_up_grad = jnp.dot(in_rows.T, grad_pu, preferred_element_type=jnp.float32).astype(jnp.bfloat16)
    w_down_grad = jnp.dot(hidden.T, grad_z, preferred_element_type=jnp.float32).astype(jnp.bfloat16)
    grad_in = jnp.dot(grad_pg, w_gate.T, preferred_element_type=jnp.float32) + jnp.dot(grad_pu, w_up.T, preferred_element_type=jnp.float32)
    x_grad = (grad_in * spread(in_scale)).astype(jnp.bfloat16)
    in_scale_grad = per_member(tokens.astype(jnp.float32) * grad_in)
    down_out = jnp.dot(hidden, w_down, preferred_element_type=jnp.float32)
    out_scale_grad = per_member(out_grad.astype(jnp.float32) * down_out)
    return (x_grad, w_gate_grad, w_up_grad, w_down_grad, in_scale_grad, out_scale_grad, gate_scale_grad, gate_flip_grad, up_scale_grad, up_flip_grad)
```

```python
import jax
import jax.numpy as jnp
from jax import lax
from jax.sharding import PartitionSpec as P


BF = jnp.bfloat16
F32 = jnp.float32


def contract_rows(left, right):
    return lax.dot_general(left, right, (((0,), (0,)), ((), ())), preferred_element_type=F32)


def contract_cols(left, right):
    return lax.dot_general(left, right, (((1,), (1,)), ((), ())), preferred_element_type=F32)


class Grid:
    def __init__(self, axis, count, inner):
        self.axis, self.count, self.inner, self.outer = axis, count, inner, count // inner
        me = lax.axis_index(axis)
        self.o, self.i = me // inner, me % inner

    def shift_outer(self, block):
        n = self.inner
        perm = [(p, ((p // n + 1) % self.outer) * n + p % n) for p in range(self.count)]
        return lax.ppermute(block, self.axis, perm)

    def shift_inner(self, block):
        n = self.inner
        perm = [(p, (p // n) * n + (p % n + 1) % n) for p in range(self.count)]
        return lax.ppermute(block, self.axis, perm)

    def sides(self, block):
        slots = [block]
        for _ in range(1, self.inner):
            slots.append(self.shift_inner(slots[-1]))
        return slots

    def gather(self, block):
        slots = self.sides(block)
        for _ in range(1, self.outer):
            block = self.shift_outer(block)
            slots += self.sides(block)
        return slots

    def swap_order(self, array):
        picks = []
        for k in range(self.outer):
            for e in range(self.inner):
                place = ((self.o - k) % self.outer) * self.inner + (self.i - e) % self.inner
                picks.append(lax.dynamic_index_in_dim(array, place, 0, keepdims=True))
        return jnp.concatenate(picks, axis=0)


def spread_tensor(tensor, block):
    current, parts = block, [block]
    for _ in range(1, tensor.outer):
        current = tensor.shift_outer(current)
        parts.append(current)
    stack = jnp.stack(parts)
    pairs = [stack]
    for _ in range(1, tensor.inner):
        pairs.append(tensor.shift_inner(pairs[-1]))
    both = jnp.stack(pairs, axis=1)
    return tensor.swap_order(both.reshape((tensor.count,) + block.shape))


def to_width(tensor, block, members):
    rows = block.shape[0]
    piece = rows // tensor.count
    mine = lax.dynamic_slice_in_dim(block, lax.axis_index("tensor") * piece, piece, 0)
    swapped = lax.all_to_all(mine, "member", split_axis=1, concat_axis=0, tiled=True)
    width = swapped.shape[1]
    spread = spread_tensor(tensor, swapped.reshape(members, piece, width))
    return spread.transpose(1, 0, 2, 3).reshape(members, rows, width)


def local(
    tokens,
    out_grad,
    flip_bits,
    in_scale,
    out_scale,
    gate_scale,
    gate_flip,
    up_scale,
    up_flip,
    proj_gate,
    proj_up,
    w_gate,
    w_up,
    w_down,
):
    rows = tokens.shape[0]
    members, width = in_scale.shape
    count = lax.axis_size("tensor")
    outer = 4 if members % 4 == 0 else 1
    grid = Grid("member", members, members // outer)
    tensor = Grid("tensor", count, 2 if count % 2 == 0 else 1)
    inner = grid.inner

    sign = (2 * flip_bits - 1).astype(F32)[:, None]
    gate_factor = gate_scale + sign * gate_flip
    up_factor = up_scale + sign * up_flip
    pg_f = proj_gate.astype(F32)
    pu_f = proj_up.astype(F32)
    gate = pg_f * gate_factor
    up = pu_f * up_factor
    sig = jax.nn.sigmoid(gate)
    act = gate * sig
    hidden = (act * up).astype(BF)

    hid_slots = grid.sides(hidden)
    next_hidden = grid.shift_outer(hidden)
    cotan = to_width(tensor, out_grad, members)
    cotan, next_hidden, hid_slots = lax.optimization_barrier((cotan, next_hidden, hid_slots))
    cotan = grid.swap_order(cotan)
    out_table = grid.swap_order(out_scale)
    in_table = grid.swap_order(in_scale)
    grad_z = (cotan.astype(F32) * out_table[:, None, :]).astype(BF)

    total = None
    for k in list(range(1, outer)) + [0]:
        group = grad_z[k * inner : (k + 1) * inner]
        part = contract_cols(group.reshape(inner * rows, width), w_down).reshape(inner, rows, -1)
        if inner > 1:
            side = part[1].astype(BF)
            for e in range(2, inner):
                side = (grid.shift_inner(side).astype(F32) + part[e]).astype(BF)
            near = part[0] + grid.shift_inner(side).astype(F32)
        else:
            near = part[0]
        if total is not None:
            near = near + grid.shift_outer(total.astype(BF)).astype(F32)
        total = near
    grad_hidden = total

    grad_gate = grad_hidden * up * sig * (1.0 + gate * (1.0 - sig))
    grad_up = grad_hidden * act
    gate_scale_grad = jnp.sum(grad_gate * pg_f, axis=0, keepdims=True)
    gate_flip_grad = jnp.sum(sign * grad_gate * pg_f, axis=0, keepdims=True)
    up_scale_grad = jnp.sum(grad_up * pu_f, axis=0, keepdims=True)
    up_flip_grad = jnp.sum(sign * grad_up * pu_f, axis=0, keepdims=True)
    grad_pg = (grad_gate * gate_factor).astype(BF)
    grad_pu = (grad_up * up_factor).astype(BF)

    pg_slots = grid.gather(grad_pg)
    pu_slots = grid.gather(grad_pu)
    next_hidden, _ = lax.optimization_barrier((next_hidden, pu_slots[-inner]))
    hid_slots += grid.sides(next_hidden)
    for _ in range(2, outer):
        next_hidden = grid.shift_outer(next_hidden)
        hid_slots += grid.sides(next_hidden)

    all_tokens = grid.swap_order(to_width(tensor, tokens, members))
    in_rows = (all_tokens.astype(F32) * in_table[:, None, :]).astype(BF)
    in_rows = in_rows.reshape(members * rows, width)
    grad_z = grad_z.reshape(members * rows, width)

    hid = jnp.concatenate(hid_slots, axis=0)
    down_acc = contract_rows(hid, grad_z).astype(BF)
    down_out = jnp.dot(hid, w_down, preferred_element_type=F32).reshape(members, rows, width)
    out_part = grid.swap_order((cotan.astype(F32) * down_out).sum(axis=1))
    out_scale_grad = spread_tensor(tensor, out_part).sum(axis=0)

    pg = jnp.concatenate(pg_slots, axis=0)
    gate_acc = contract_rows(in_rows, pg).astype(BF)
    grad_in = contract_cols(pg, w_gate)
    pu = jnp.concatenate(pu_slots, axis=0)
    grad_in = (grad_in + contract_cols(pu, w_up)).reshape(members, rows, width)
    up_acc = contract_rows(in_rows, pu).astype(BF)

    in_part = grid.swap_order((all_tokens.astype(F32) * grad_in).sum(axis=1))
    in_scale_grad = spread_tensor(tensor, in_part).sum(axis=0)

    piece = rows // count
    scaled = grad_in * in_table[:, None, :]
    scaled = scaled.reshape(members, tensor.outer, tensor.inner, piece, width)
    if tensor.inner > 1:
        away = lax.dynamic_index_in_dim(scaled, 1 - tensor.i, 2, keepdims=False).astype(BF)
        keep = lax.dynamic_index_in_dim(scaled, tensor.i, 2, keepdims=False)
        near = keep + tensor.shift_inner(away).astype(F32)
    else:
        near = scaled[:, :, 0]
    summed = None
    for k in list(range(1, tensor.outer)) + [0]:
        own = lax.dynamic_index_in_dim(near, (tensor.o - k) % tensor.outer, 1, keepdims=False)
        if summed is not None:
            own = own + tensor.shift_outer(summed.astype(BF)).astype(F32)
        summed = own
    summed = grid.swap_order(summed.astype(BF))
    returned = lax.all_to_all(summed, "member", split_axis=0, concat_axis=2, tiled=True)
    x_grad = returned.reshape(piece, members * width)
    return (
        x_grad,
        gate_acc,
        up_acc,
        down_acc,
        in_scale_grad,
        out_scale_grad,
        gate_scale_grad,
        gate_flip_grad,
        up_scale_grad,
        up_flip_grad,
    )


def solution(mesh):
    return jax.shard_map(
        local,
        mesh=mesh,
        in_specs=(
            P("member", None),
            P("member", None),
            P("member"),
            P(None, "member"),
            P(None, "member"),
            P("member", "tensor"),
            P("member", "tensor"),
            P("member", "tensor"),
            P("member", "tensor"),
            P("member", "tensor"),
            P("member", "tensor"),
            P("member", "tensor"),
            P("member", "tensor"),
            P("tensor", "member"),
        ),
        out_specs=(
            P(("member", "tensor"), None),
            P("member", "tensor"),
            P("member", "tensor"),
            P("tensor", "member"),
            P(None, "member"),
            P(None, "member"),
            P("member", "tensor"),
            P("member", "tensor"),
            P("member", "tensor"),
            P("member", "tensor"),
        ),
        check_vma=False,
    )
```

```python
import jax
import jax.numpy as jnp
from jax import lax
from jax.sharding import PartitionSpec as P


BF = jnp.bfloat16
F32 = jnp.float32


def contract_rows(left, right):
    return lax.dot_general(left, right, (((0,), (0,)), ((), ())), preferred_element_type=F32)


def contract_cols(left, right):
    return lax.dot_general(left, right, (((1,), (1,)), ((), ())), preferred_element_type=F32)


class Grid:
    def __init__(self, axis, count, inner):
        self.axis, self.count, self.inner, self.outer = axis, count, inner, count // inner
        me = lax.axis_index(axis)
        self.o, self.i = me // inner, me % inner

    def shift_outer(self, block):
        n = self.inner
        perm = [(p, ((p // n + 1) % self.outer) * n + p % n) for p in range(self.count)]
        return lax.ppermute(block, self.axis, perm)

    def shift_inner(self, block):
        n = self.inner
        perm = [(p, (p // n) * n + (p % n + 1) % n) for p in range(self.count)]
        return lax.ppermute(block, self.axis, perm)

    def sides(self, block):
        slots = [block]
        for _ in range(1, self.inner):
            slots.append(self.shift_inner(slots[-1]))
        return slots

    def gather(self, block):
        slots = self.sides(block)
        for _ in range(1, self.outer):
            block = self.shift_outer(block)
            slots += self.sides(block)
        return slots

    def swap_order(self, array):
        picks = []
        for k in range(self.outer):
            for e in range(self.inner):
                place = ((self.o - k) % self.outer) * self.inner + (self.i - e) % self.inner
                picks.append(lax.dynamic_index_in_dim(array, place, 0, keepdims=True))
        return jnp.concatenate(picks, axis=0)


def spread_tensor(tensor, block):
    current, parts = block, [block]
    for _ in range(1, tensor.outer):
        current = tensor.shift_outer(current)
        parts.append(current)
    stack = jnp.stack(parts)
    pairs = [stack]
    for _ in range(1, tensor.inner):
        pairs.append(tensor.shift_inner(pairs[-1]))
    both = jnp.stack(pairs, axis=1)
    return tensor.swap_order(both.reshape((tensor.count,) + block.shape))


def to_width(tensor, block, members):
    rows = block.shape[0]
    piece = rows // tensor.count
    mine = lax.dynamic_slice_in_dim(block, lax.axis_index("tensor") * piece, piece, 0)
    swapped = lax.all_to_all(mine, "member", split_axis=1, concat_axis=0, tiled=True)
    width = swapped.shape[1]
    spread = spread_tensor(tensor, swapped.reshape(members, piece, width))
    return spread.transpose(1, 0, 2, 3).reshape(members, rows, width)


def local(
    tokens,
    out_grad,
    flip_bits,
    in_scale,
    out_scale,
    gate_scale,
    gate_flip,
    up_scale,
    up_flip,
    proj_gate,
    proj_up,
    w_gate,
    w_up,
    w_down,
):
    rows = tokens.shape[0]
    members, width = in_scale.shape
    count = lax.axis_size("tensor")
    outer = 4 if members % 4 == 0 else 1
    grid = Grid("member", members, members // outer)
    tensor = Grid("tensor", count, 2 if count % 2 == 0 else 1)
    inner = grid.inner

    sign = (2 * flip_bits - 1).astype(F32)[:, None]
    gate_factor = gate_scale + sign * gate_flip
    up_factor = up_scale + sign * up_flip
    pg_f = proj_gate.astype(F32)
    pu_f = proj_up.astype(F32)
    gate = pg_f * gate_factor
    up = pu_f * up_factor
    sig = jax.nn.sigmoid(gate)
    act = gate * sig
    hidden = (act * up).astype(BF)

    hidden, out_grad = lax.optimization_barrier((hidden, out_grad))
    hid_hop = grid.sides(hidden)
    next_hidden = grid.shift_outer(hidden)
    hid_slots = list(hid_hop)
    cotan = to_width(tensor, out_grad, members)
    cotan, next_hidden, hid_hop = lax.optimization_barrier((cotan, next_hidden, hid_hop))
    cotan = grid.swap_order(cotan)
    out_table = grid.swap_order(out_scale)
    in_table = grid.swap_order(in_scale)
    grad_z = (cotan.astype(F32) * out_table[:, None, :]).astype(BF)

    total = None
    for k in list(range(1, outer)) + [0]:
        group = grad_z[k * inner : (k + 1) * inner]
        part = contract_cols(group.reshape(inner * rows, width), w_down).reshape(inner, rows, -1)
        if inner > 1:
            side = part[1].astype(BF)
            for e in range(2, inner):
                side = (grid.shift_inner(side).astype(F32) + part[e]).astype(BF)
            near = part[0] + grid.shift_inner(side).astype(F32)
        else:
            near = part[0]
        if total is not None:
            near = near + grid.shift_outer(total.astype(BF)).astype(F32)
        total = near
    grad_hidden = total

    grad_gate = grad_hidden * up * sig * (1.0 + gate * (1.0 - sig))
    grad_up = grad_hidden * act
    gate_scale_grad = jnp.sum(grad_gate * pg_f, axis=0, keepdims=True)
    gate_flip_grad = jnp.sum(sign * grad_gate * pg_f, axis=0, keepdims=True)
    up_scale_grad = jnp.sum(grad_up * pu_f, axis=0, keepdims=True)
    up_flip_grad = jnp.sum(sign * grad_up * pu_f, axis=0, keepdims=True)
    grad_pg = (grad_gate * gate_factor).astype(BF)
    grad_pu = (grad_up * up_factor).astype(BF)

    tokens, grad_pg = lax.optimization_barrier((tokens, grad_pg))
    pg_slots = grid.gather(grad_pg)
    grad_pu, _ = lax.optimization_barrier((grad_pu, pg_slots[-inner]))
    pu_slots = grid.gather(grad_pu)
    hid_hop = [next_hidden] + [grid.shift_outer(side) for side in hid_hop[1:]]
    hid_hop, _ = lax.optimization_barrier((hid_hop, pu_slots[inner]))
    hid_slots += hid_hop
    for _ in range(2, outer - 1):
        hid_hop = [grid.shift_outer(side) for side in hid_hop]
        hid_slots += hid_hop
    hid_slots += grid.sides(grid.shift_outer(hid_hop[0]))

    all_tokens = grid.swap_order(to_width(tensor, tokens, members))
    in_rows = (all_tokens.astype(F32) * in_table[:, None, :]).astype(BF)
    in_rows = in_rows.reshape(members * rows, width)
    grad_z = grad_z.reshape(members * rows, width)

    hid = jnp.concatenate(hid_slots, axis=0)
    down_acc = contract_rows(hid, grad_z).astype(BF)
    down_out = jnp.dot(hid, w_down, preferred_element_type=F32).reshape(members, rows, width)
    out_part = grid.swap_order((cotan.astype(F32) * down_out).sum(axis=1))
    out_scale_grad = spread_tensor(tensor, out_part).sum(axis=0)

    pg = jnp.concatenate(pg_slots, axis=0)
    gate_acc = contract_rows(in_rows, pg).astype(BF)
    grad_in = contract_cols(pg, w_gate)
    pu = jnp.concatenate(pu_slots, axis=0)
    grad_in = (grad_in + contract_cols(pu, w_up)).reshape(members, rows, width)
    up_acc = contract_rows(in_rows, pu).astype(BF)

    in_part = grid.swap_order((all_tokens.astype(F32) * grad_in).sum(axis=1))
    in_scale_grad = spread_tensor(tensor, in_part).sum(axis=0)

    piece = rows // count
    scaled = grad_in * in_table[:, None, :]
    scaled = scaled.reshape(members, tensor.outer, tensor.inner, piece, width)
    if tensor.inner > 1:
        away = lax.dynamic_index_in_dim(scaled, 1 - tensor.i, 2, keepdims=False).astype(BF)
        keep = lax.dynamic_index_in_dim(scaled, tensor.i, 2, keepdims=False)
        near = keep + tensor.shift_inner(away).astype(F32)
    else:
        near = scaled[:, :, 0]
    summed = None
    for k in list(range(1, tensor.outer)) + [0]:
        own = lax.dynamic_index_in_dim(near, (tensor.o - k) % tensor.outer, 1, keepdims=False)
        if summed is not None:
            own = own + tensor.shift_outer(summed.astype(BF)).astype(F32)
        summed = own
    summed = grid.swap_order(summed.astype(BF))
    returned = lax.all_to_all(summed, "member", split_axis=0, concat_axis=2, tiled=True)
    x_grad = returned.reshape(piece, members * width)
    return (
        x_grad,
        gate_acc,
        up_acc,
        down_acc,
        in_scale_grad,
        out_scale_grad,
        gate_scale_grad,
        gate_flip_grad,
        up_scale_grad,
        up_flip_grad,
    )


def solution(mesh):
    return jax.shard_map(
        local,
        mesh=mesh,
        in_specs=(
            P("member", None),
            P("member", None),
            P("member"),
            P(None, "member"),
            P(None, "member"),
            P("member", "tensor"),
            P("member", "tensor"),
            P("member", "tensor"),
            P("member", "tensor"),
            P("member", "tensor"),
            P("member", "tensor"),
            P("member", "tensor"),
            P("member", "tensor"),
            P("tensor", "member"),
        ),
        out_specs=(
            P(("member", "tensor"), None),
            P("member", "tensor"),
            P("member", "tensor"),
            P("tensor", "member"),
            P(None, "member"),
            P(None, "member"),
            P("member", "tensor"),
            P("member", "tensor"),
            P("member", "tensor"),
            P("member", "tensor"),
        ),
        check_vma=False,
    )
```
